32 devices in a mesh: row: 4 (over y, core), col: 8 (over z, x).
Axes of the slice: x: 2, y: 2, z: 4, core: 2. Of those that a mesh axis runs over, the one named last changes fastest.
Arguments:
- calib: bfloat16 [256, 8192], replicated, may hold values from -6 to 6
- gate_a: bfloat16 [8192, 28672], P('col', 'row'), may hold values from -0.0625 to 0.0625
- up_a: bfloat16 [8192, 28672], P('col', 'row'), may hold values from -0.0625 to 0.0625
- gate_b: bfloat16 [8192, 28672], P('row', 'col'), may hold values from -0.0625 to 0.0625
- up_b: bfloat16 [8192, 28672], P('row', 'col'), may hold values from -0.0625 to 0.0625
- down_a: bfloat16 [28672, 1024], P(('row', 'col')), may hold values from -6 to 6
- down_b: bfloat16 [28672, 1024], P('col', 'row'), may hold values from -6 to 6
Outputs:
- joined: bfloat16 [28672, 1024], P(('row', 'col'))
The draws below stay inside these ranges and needn't reach their ends.
All inputs are finite; a program needn't handle non-finite values.
Results may differ from the reference program's by a relative error of at most 0.025.
Values may be sent and summed in bfloat16 or wider, within the bound.
A program may use at most 384 MiB of HBM per device.

```python
import jax
import jax.numpy as jnp
from jax import lax

D = 8192
FF = 28672
CALIB_TOKENS = 256
DW = 1024
ITERS = 3
BLOCK_B = 3584
N_ROW = 4
N_COL = 8


def levels(rng, shape, shards, low, high):
    def one(dim, blocks):
        draws = jax.random.uniform(jax.random.fold_in(jax.random.fold_in(rng, 6), dim), (blocks,), jnp.float32, low / len(shards), high / len(shards))
        return jnp.repeat(jnp.exp(draws), shape[dim] // blocks).reshape((-1,) + (1,) * (len(shape) - dim - 1))

    level = one(*shards[0])
    for cut in shards[1:]:
        level = level * one(*cut)
    return level


def scatter_about(key, extent, deviation, reach, pieces=(), held_as=jnp.bfloat16):
    values = deviation * jax.random.normal(key, extent, jnp.float32)
    if pieces:
        values = values * levels(key, extent, pieces, -0.22, 0.18)
    return jnp.clip(values, -reach, reach).astype(held_as)


def setup_inputs(seed: int = 0) -> dict:
    keys = jax.random.split(jax.random.key(seed), 8)
    return {
        "calib": scatter_about(keys[0], (CALIB_TOKENS, D), 1.0, 6.0),
        "gate_a": scatter_about(keys[1], (D, FF), D ** -0.5, 0.0625, ((0, 8), (1, 4))),
        "up_a": scatter_about(keys[2], (D, FF), D ** -0.5, 0.0625, ((0, 8), (1, 4))),
        "gate_b": scatter_about(keys[3], (D, FF), D ** -0.5, 0.0625, ((0, 4), (1, 8))),
        "up_b": scatter_about(keys[4], (D, FF), D ** -0.5, 0.0625, ((0, 4), (1, 8))),
        "down_a": scatter_about(keys[5], (FF, DW), 1.0, 6.0, ((0, 32),)),
        "down_b": scatter_about(keys[6], (FF, DW), 1.0, 6.0, ((0, 8), (1, 4))),
    }


softness = 0.02
statistic_floor = 1e-05

def standardize(gate_pre, up_preactivation):
    hidden = jax.nn.silu(gate_pre) * up_preactivation
    center = lax.optimization_barrier(jnp.mean(hidden, axis=0, keepdims=True))
    spread = lax.optimization_barrier(jnp.mean(jnp.square(hidden - center), axis=0, keepdims=True))
    return ((hidden - center) * lax.rsqrt(spread + statistic_floor)).astype(jnp.bfloat16)

def reference(calib, gate_a, up_a, gate_b, up_b, down_a, down_b):
    first_model_scores = standardize(jnp.dot(calib, gate_a, preferred_element_type=jnp.float32), jnp.dot(calib, up_a, preferred_element_type=jnp.float32))
    scores_b = standardize(jnp.dot(calib, gate_b, preferred_element_type=jnp.float32), jnp.dot(calib, up_b, preferred_element_type=jnp.float32))
    row_block = FF // N_ROW
    multiplier = 1.0 / (CALIB_TOKENS * softness)

    def kernel_rows(index):
        start = (index * row_block).astype(jnp.int32)
        rows_a = lax.dynamic_slice_in_dim(first_model_scores, start, row_block, 1)
        return jnp.exp(jnp.dot(rows_a.T, scores_b, preferred_element_type=jnp.float32) * multiplier)
    kernel = lax.map(kernel_rows, jnp.arange(N_ROW, dtype=jnp.int32)).reshape(FF, FF)
    column_scaling = jnp.ones((FF,), jnp.float32)
    for step in range(ITERS):
        row_scale = 1.0 / jnp.dot(kernel, column_scaling, precision=lax.Precision.HIGHEST)
        column_scaling = 1.0 / jnp.dot(row_scale, kernel, precision=lax.Precision.HIGHEST)

    def add_block(index, total):
        start = (index * BLOCK_B).astype(jnp.int32)
        kernel_cols = lax.dynamic_slice_in_dim(kernel, start, BLOCK_B, 1)
        scale_cols = lax.dynamic_slice_in_dim(column_scaling, start, BLOCK_B, 0)
        plan = (row_scale[:, None] * kernel_cols * scale_cols[None, :]).astype(jnp.bfloat16)
        rows_b = lax.dynamic_slice_in_dim(down_b, start, BLOCK_B, 0)
        part = jnp.dot(plan, rows_b, preferred_element_type=jnp.float32).astype(jnp.bfloat16)
        part = lax.optimization_barrier(part)
        return total + part.astype(jnp.float32)
    aligned = lax.fori_loop(0, N_COL, add_block, jnp.zeros((FF, DW), jnp.float32))
    return ((down_a.astype(jnp.float32) + aligned) * 0.5).astype(jnp.bfloat16)
```

```python
import functools
import math

import jax
import jax.numpy as jnp
from jax import lax
from jax.experimental import pallas as pl
from jax.experimental.pallas import tpu as pltpu
from jax.sharding import PartitionSpec as P

ITERS = 3


softness = 0.02
statistic_floor = 1e-05
LANES = 128


def standardize(gate_pre, up_preactivation):
    hidden = jax.nn.silu(gate_pre) * up_preactivation
    center = jnp.mean(hidden, axis=0, keepdims=True)
    spread = jnp.mean(jnp.square(hidden - center), axis=0, keepdims=True)
    return ((hidden - center) * lax.rsqrt(spread + statistic_floor)).astype(jnp.bfloat16)


def block_of(size, most):
    block = most
    while size % block:
        block //= 2
    return block


def lane_chunk(size, most):
    chunk = most
    while size % chunk:
        chunk -= LANES
    return chunk


MESH = pl.DeviceIdType.MESH


def grid_of(members):
    inner = 1
    while (2 * inner) ** 2 <= members and members % (2 * inner) == 0:
        inner *= 2
    return members // inner, inner


def halves_of(vector):
    high = vector.astype(jnp.bfloat16).astype(jnp.float32)
    low = vector - high
    place = lax.broadcasted_iota(jnp.int32, (16, vector.shape[1]), 0)
    return jnp.where(place == 0, high, jnp.where(place == 1, low, 0.0)).astype(jnp.bfloat16)


def sinkhorn(scores_a, scores_b, n_row, n_col, exponent):
    rows, depth = scores_a.shape
    cols = scores_b.shape[0]
    outer, inner = grid_of(n_col)
    block = block_of(rows, 512)
    chunk = lane_chunk(cols, 512)

    def body(a_ref, b_ref, r_ref, c_ref, b_all, k_ref, rv, cv, r_send, c_send, r_recv, c_recv, pair,
             rs, rr, cs, cr, bs, br, local, ps, pr):
        me_row, me_col = lax.axis_index("row"), lax.axis_index("col")
        partner = lax.rem(me_col + n_col // 2, n_col)
        barrier = pltpu.get_barrier_semaphore()
        for j in range(1, n_col):
            pl.semaphore_signal(barrier, 1, device_id={"col": lax.rem(me_col + j, n_col)}, device_id_type=MESH)
        for j in range(1, n_row):
            pl.semaphore_signal(barrier, 1, device_id={"row": lax.rem(me_row + j, n_row)}, device_id_type=MESH)
        pl.semaphore_wait(barrier, n_col + n_row - 2)

        own_b = pltpu.make_async_copy(b_ref, b_all.at[0], local)
        own_b.start()
        pair_b = pltpu.make_async_remote_copy(
            b_ref, b_all.at[1], bs, br, device_id={"col": partner}, device_id_type=MESH)
        pair_b.start()

        def swap(step, send, recv, ssem, rsem, axis, me, n):
            copies = []
            for j in range(1, n):
                copy = pltpu.make_async_remote_copy(
                    send.at[step], recv.at[step, j], ssem.at[step, j], rsem.at[step, j],
                    device_id={axis: lax.rem(me + j, n)}, device_id_type=MESH)
                copy.start()
                copies.append(copy)
            total = send[step]
            for j, copy in enumerate(copies):
                copy.wait()
                total = total + recv[step, j + 1]
            return 1.0 / total

        def row_part(step, base):
            part = lax.dot_general(
                cv[...], k_ref[pl.ds(base, block), :], (((1,), (1,)), ((), ())),
                preferred_element_type=jnp.float32)
            r_send[step, :, pl.ds(base, block)] = part[0:1] + part[1:2]

        cv[...] = halves_of(jnp.ones((1, cols), jnp.float32))

        @pl.loop(0, rows // block)
        def _(i):
            base = pl.multiple_of(i * block, block)
            for start in range(0, cols, chunk):
                logits = lax.dot_general(
                    a_ref[pl.ds(base, block), :], b_ref[start : start + chunk, :], (((1,), (1,)), ((), ())),
                    preferred_element_type=jnp.float32)
                k_ref[pl.ds(base, block), start : start + chunk] = jnp.exp2(logits * exponent).astype(jnp.bfloat16)
            row_part(0, base)

        for step in range(ITERS):
            if step:
                @pl.loop(0, rows // block)
                def _(i):
                    row_part(step, pl.multiple_of(i * block, block))
            scale = swap(step, r_send, r_recv, rs, rr, "col", me_col, n_col)
            rv[...] = halves_of(scale)
            if step == ITERS - 1:
                r_ref[...] = scale
            c_send[step] = jnp.zeros((1, cols), jnp.float32)

            @pl.loop(0, rows // block)
            def _(i):
                base = pl.multiple_of(i * block, block)
                part = jnp.dot(
                    rv[:, pl.ds(base, block)], k_ref[pl.ds(base, block), :], preferred_element_type=jnp.float32)
                c_send[step] += part[0:1] + part[1:2]

            scale = swap(step, c_send, c_recv, cs, cr, "row", me_row, n_row)
            if step < ITERS - 1:
                cv[...] = halves_of(scale)
            else:
                pair[0] = scale
                pair_c = pltpu.make_async_remote_copy(
                    pair.at[0], pair.at[1], ps, pr, device_id={"col": partner}, device_id_type=MESH)
                pair_c.start()
                pair_c.wait()
                c_ref[...] = pair[...]
        own_b.wait()
        pair_b.wait()

    dma = pltpu.SemaphoreType.DMA
    return pl.pallas_call(
        body,
        in_specs=[pl.BlockSpec(memory_space=pltpu.VMEM)] * 2,
        out_specs=[
            pl.BlockSpec(memory_space=pltpu.VMEM),
            pl.BlockSpec(memory_space=pltpu.VMEM),
            pl.BlockSpec(memory_space=pl.ANY),
        ],
        out_shape=[
            jax.ShapeDtypeStruct((1, rows), jnp.float32),
            jax.ShapeDtypeStruct((2, 1, cols), jnp.float32),
            jax.ShapeDtypeStruct((2, cols, depth), jnp.bfloat16),
        ],
        scratch_shapes=[
            pltpu.VMEM((rows, cols), jnp.bfloat16),
            pltpu.VMEM((16, rows), jnp.bfloat16),
            pltpu.VMEM((16, cols), jnp.bfloat16),
            pltpu.VMEM((ITERS, 1, rows), jnp.float32),
            pltpu.VMEM((ITERS, 1, cols), jnp.float32),
            pltpu.VMEM((ITERS, n_col, 1, rows), jnp.float32),
            pltpu.VMEM((ITERS, n_row, 1, cols), jnp.float32),
            pltpu.VMEM((2, 1, cols), jnp.float32),
            dma((ITERS, n_col)), dma((ITERS, n_col)), dma((ITERS, n_row)), dma((ITERS, n_row)),
            dma, dma, dma, dma, dma,
        ],
        compiler_params=pltpu.CompilerParams(
            collective_id=1, has_side_effects=True, vmem_limit_bytes=67043328),
        cost_estimate=pl.CostEstimate(
            flops=2 * rows * cols * depth * 3, bytes_accessed=2 * (rows + cols) * depth, transcendentals=rows * cols),
        name="sinkhorn",
    )(scores_a, scores_b)


def join(scores_a, b_all, row_scale, col_scale, down_own, down_pair, down_a, n_col, exponent):
    rows, depth = scores_a.shape
    cols = b_all.shape[1]
    quarters, _, width = down_own.shape
    window = quarters * width
    outer, inner = grid_of(n_col)
    near = outer // 2
    group = near * inner
    half, own = rows // 2, rows // n_col
    subs = 2
    piece = own // subs
    steps = group * subs
    sent = steps - subs
    chunk = lane_chunk(cols, 512)
    pieces = cols // chunk

    def body(a_hbm, b_hbm, r_ref, c_ref, own_hbm, pair_hbm, down_ref, out_ref, a_ref, b_ref, d_ref, total, plan,
             out_buf, in_buf, local, ssem, rsem):
        me = lax.axis_index("col")
        mo, mi = me // inner, lax.rem(me, inner)
        side, near_o = mo // near, lax.rem(mo, near)

        def place(j):
            oo = lax.rem(near_o + j // inner, near)
            ii = lax.rem(mi + lax.rem(j, inner), inner)
            return (side * near + oo) * inner + ii

        barrier = pltpu.get_barrier_semaphore()
        for j in range(1, group):
            pl.semaphore_signal(barrier, 1, device_id={"col": place(j)}, device_id_type=MESH)
        loads = [
            pltpu.make_async_copy(a_hbm.at[pl.ds(pl.multiple_of(side * half, 8), half)], a_ref, local.at[0]),
            pltpu.make_async_copy(b_hbm, b_ref, local.at[1]),
            pltpu.make_async_copy(own_hbm, d_ref.at[0], local.at[2]),
            pltpu.make_async_copy(pair_hbm, d_ref.at[1], local.at[3]),
        ]
        for load in loads:
            load.start()
        for load in loads:
            load.wait()
        pl.semaphore_wait(barrier, group - 1)

        def copy_of(t, target):
            return pltpu.make_async_remote_copy(
                out_buf.at[t], in_buf.at[t], ssem.at[t], rsem.at[t],
                device_id={"col": target}, device_id_type=MESH)

        @pl.loop(0, steps)
        def _(t):
            j = (group - 1) - t // subs
            target = place(j)
            first = pl.multiple_of((target - side * group) * own + lax.rem(t, subs) * piece, math.gcd(piece, 128))
            total[...] = jnp.zeros_like(total)
            for s in range(2):
                @pl.loop(0, pieces)
                def _(k):
                    base = pl.multiple_of(k * chunk, chunk)
                    logits = lax.dot_general(
                        a_ref[pl.ds(first, piece), :], b_ref[s, pl.ds(base, chunk), :], (((1,), (1,)), ((), ())),
                        preferred_element_type=jnp.float32)
                    plan[...] = (jnp.exp2(logits * exponent) * c_ref[s, :, pl.ds(base, chunk)]).astype(jnp.bfloat16)
                    for q in range(quarters):
                        total[:, q * width : (q + 1) * width] += jnp.dot(
                            plan[...], d_ref[s, q, pl.ds(base, chunk), :], preferred_element_type=jnp.float32)
            spot = pl.multiple_of(target * own + lax.rem(t, subs) * piece, math.gcd(piece, 8))
            out_buf[t] = (total[...] * r_ref[pl.ds(spot, piece), :]).astype(jnp.bfloat16)

            @pl.when(t < sent)
            def _():
                copy_of(t, target).start()

        @pl.loop(0, subs)
        def _(u):
            summed = out_buf[sent + u].astype(jnp.float32)
            for g in range(group - 1):
                copy_of(g * subs + u, place(1)).wait_recv()
                summed = summed + in_buf[g * subs + u].astype(jnp.float32)
            spot = pl.ds(pl.multiple_of(u * piece, math.gcd(piece, 16)), piece)
            out_ref[spot, :] = ((down_ref[spot, :].astype(jnp.float32) + summed) * 0.5).astype(jnp.bfloat16)

        @pl.loop(0, sent)
        def _(t):
            copy_of(t, place((group - 1) - t // subs)).wait_send()

    dma = pltpu.SemaphoreType.DMA
    vmem, hbm = pl.BlockSpec(memory_space=pltpu.VMEM), pl.BlockSpec(memory_space=pl.ANY)
    return pl.pallas_call(
        body,
        in_specs=[hbm, hbm, vmem, vmem, hbm, hbm, vmem],
        out_specs=vmem,
        out_shape=jax.ShapeDtypeStruct((own, window), jnp.bfloat16),
        scratch_shapes=[
            pltpu.VMEM((half, depth), jnp.bfloat16),
            pltpu.VMEM((2, cols, depth), jnp.bfloat16),
            pltpu.VMEM((2, quarters, cols, width), jnp.bfloat16),
            pltpu.VMEM((piece, window), jnp.float32),
            pltpu.VMEM((piece, chunk), jnp.bfloat16),
            pltpu.VMEM((steps, piece, window), jnp.bfloat16),
            pltpu.VMEM((sent, piece, window), jnp.bfloat16),
            dma((4,)), dma((steps,)), dma((steps,)),
        ],
        compiler_params=pltpu.CompilerParams(
            collective_id=2, has_side_effects=True, vmem_limit_bytes=67043328),
        cost_estimate=pl.CostEstimate(
            flops=2 * rows * cols * (window + depth), bytes_accessed=8 * cols * window, transcendentals=rows * cols),
        name="join",
    )(scores_a, b_all, row_scale, col_scale, down_own, down_pair, down_a)


def reduced(gate_pre, up_pre, axis, parts):
    tokens, width = gate_pre.shape
    own = width // parts
    both = jnp.stack((gate_pre.astype(jnp.bfloat16), up_pre.astype(jnp.bfloat16)))
    both = both.reshape(2, tokens, parts, own).transpose(2, 0, 1, 3)
    return lax.psum_scatter(both, axis, scatter_dimension=0, tiled=False)


def scores_of(summed, axis):
    summed = summed.astype(jnp.float32)
    mine = standardize(summed[0], summed[1]).T
    return lax.all_gather(mine, axis, axis=0, tiled=True)


def solution(mesh):
    n_row, n_col = mesh.shape["row"], mesh.shape["col"]

    def per_device(calib, gate_a, up_a, gate_b, up_b, down_a, down_b):
        width_a = gate_a.shape[0]
        width_b = gate_b.shape[0]
        inputs_a = lax.dynamic_slice_in_dim(calib, lax.axis_index("col") * width_a, width_a, 1)
        inputs_b = lax.dynamic_slice_in_dim(calib, lax.axis_index("row") * width_b, width_b, 1)
        gate_pre_a = jnp.dot(inputs_a, gate_a, preferred_element_type=jnp.float32)
        up_pre_a = jnp.dot(inputs_a, up_a, preferred_element_type=jnp.float32)
        gate_pre_b = jnp.dot(inputs_b, gate_b, preferred_element_type=jnp.float32)
        up_pre_b = jnp.dot(inputs_b, up_b, preferred_element_type=jnp.float32)
        turned = [(i, (i + n_col // 2) % n_col) for i in range(n_col)]
        pair_b = lax.ppermute(down_b, "col", turned)
        summed_a = reduced(gate_pre_a, up_pre_a, "col", n_col)
        summed_a, pair_b = lax.optimization_barrier((summed_a, pair_b))
        scores_a = scores_of(summed_a, "col")
        scores_b = scores_of(reduced(gate_pre_b, up_pre_b, "row", n_row), "row")
        down_own = lax.all_gather(down_b, "row")
        down_pair = lax.all_gather(pair_b, "row")
        exponent = math.log2(math.e) / (calib.shape[0] * softness)
        row_scale, col_scale, b_all = sinkhorn(scores_a, scores_b, n_row, n_col, exponent)
        return join(
            scores_a, b_all, row_scale.reshape(-1, 1), col_scale, down_own, down_pair, down_a, n_col, exponent)

    placed = (
        P(),
        P("col", "row"),
        P("col", "row"),
        P("row", "col"),
        P("row", "col"),
        P(("row", "col"), None),
        P("col", "row"),
    )
    return jax.shard_map(
        per_device, mesh=mesh, in_specs=placed, out_specs=P(("row", "col"), None), check_vma=False
    )
```

```python
import functools
import math

import jax
import jax.numpy as jnp
from jax import lax
from jax.experimental import pallas as pl
from jax.experimental.pallas import tpu as pltpu
from jax.sharding import PartitionSpec as P

ITERS = 3


softness = 0.02
statistic_floor = 1e-05
LANES = 128


def standardize(gate_pre, up_preactivation):
    hidden = jax.nn.silu(gate_pre) * up_preactivation
    center = jnp.mean(hidden, axis=0, keepdims=True)
    spread = jnp.mean(jnp.square(hidden - center), axis=0, keepdims=True)
    return ((hidden - center) * lax.rsqrt(spread + statistic_floor)).astype(jnp.bfloat16)


def block_of(size, most):
    block = most
    while size % block:
        block //= 2
    return block


def lane_chunk(size, most):
    chunk = most
    while size % chunk:
        chunk -= LANES
    return chunk


MESH = pl.DeviceIdType.MESH


def grid_of(members):
    inner = 1
    while (2 * inner) ** 2 <= members and members % (2 * inner) == 0:
        inner *= 2
    return members // inner, inner


def halves_of(vector):
    high = vector.astype(jnp.bfloat16).astype(jnp.float32)
    low = vector - high
    place = lax.broadcasted_iota(jnp.int32, (16, vector.shape[1]), 0)
    return jnp.where(place == 0, high, jnp.where(place == 1, low, 0.0)).astype(jnp.bfloat16)


def sinkhorn(mine_a, mine_b, down_b, n_row, n_col, exponent):
    own, depth = mine_a.shape
    own_b = mine_b.shape[0]
    cols, width = down_b.shape
    rows = own * n_col
    outer, inner = grid_of(n_col)
    row_outer, row_inner = grid_of(n_row)
    block = block_of(rows, 512)
    chunk = lane_chunk(cols, 512)
    fused = own % LANES == 0
    cut = cols // 2

    def body(a_ref, b_ref, down_ref, r_ref, c_ref, a_out, b_all, d_pair, k_ref, a_all, b_own, rv, cv,
             r_send, c_send, r_recv, c_recv, pair, rs, rr, cs, cr, gs, gr, zs, zr, xs, xr,
             hs, hr, ys, yr, ks, kr, local):
        me_row, me_col = lax.axis_index("row"), lax.axis_index("col")
        partner = lax.rem(me_col + n_col // 2, n_col)
        mo, mi = me_col // inner, lax.rem(me_col, inner)
        ro, ri = me_row // row_inner, lax.rem(me_row, row_inner)
        barrier = pltpu.get_barrier_semaphore()
        for j in range(1, n_col):
            pl.semaphore_signal(barrier, 1, device_id={"col": lax.rem(me_col + j, n_col)}, device_id_type=MESH)
        for j in range(1, n_row):
            pl.semaphore_signal(barrier, 1, device_id={"row": lax.rem(me_row + j, n_row)}, device_id_type=MESH)
        keep_a = pltpu.make_async_copy(a_ref, a_all.at[me_col], local.at[0])
        keep_b = pltpu.make_async_copy(b_ref, b_own.at[me_row], local.at[1])
        keep_a.start()
        keep_b.start()
        pl.semaphore_wait(barrier, n_col + n_row - 2)

        def remote(src, dst, ssem, rsem, axis, target):
            copy = pltpu.make_async_remote_copy(
                src, dst, ssem, rsem, device_id={axis: target}, device_id_type=MESH)
            copy.start()
            return copy

        sends = []
        along, across = [], {}
        for j in range(1, outer):
            along.append(remote(a_ref, a_all.at[me_col], zs.at[j], zr.at[j], "col",
                                lax.rem(mo + j, outer) * inner + mi))
        for i in range(1, inner):
            across[0, i] = remote(a_ref, a_all.at[me_col], xs.at[0, i], xr.at[0, i], "col",
                                  mo * inner + lax.rem(mi + i, inner))
        gather_b = [
            remote(b_ref, b_own.at[me_row], gs.at[j], gr.at[j], "row", lax.rem(me_row + j, n_row))
            for j in range(1, n_row)
        ]

        def source(j, i):
            return lax.rem(mo + outer - j, outer) * inner + lax.rem(mi + inner - i, inner)

        def pass_on(j):
            along[j - 1].wait_recv()
            spot = source(j, 0)
            for i in range(1, inner):
                across[j, i] = remote(a_all.at[spot], a_all.at[spot], xs.at[j, i], xr.at[j, i], "col",
                                      mo * inner + lax.rem(mi + i, inner))

        cv[...] = halves_of(jnp.ones((1, cols), jnp.float32))

        def row_part(step, base, size):
            part = lax.dot_general(
                cv[...], k_ref[pl.ds(base, size), :], (((1,), (1,)), ((), ())),
                preferred_element_type=jnp.float32)
            r_send[step, :, pl.ds(base, size)] = part[0:1] + part[1:2]

        def build(spot):
            base = pl.multiple_of(spot * own, math.gcd(own, 128))
            if own_b % LANES == 0:
                span = LANES if own_b % 256 else 256
                per = own_b // span

                @pl.loop(0, n_row * per)
                def _(n):
                    m, inside = n // per, lax.rem(n, per)
                    logits = lax.dot_general(
                        a_all[spot], b_own[m, pl.ds(pl.multiple_of(inside * span, span), span), :],
                        (((1,), (1,)), ((), ())), preferred_element_type=jnp.float32)
                    k_ref[pl.ds(base, own), pl.ds(pl.multiple_of(n * span, span), span)] = jnp.exp2(
                        logits * exponent).astype(jnp.bfloat16)
            else:
                for m in range(n_row):
                    logits = lax.dot_general(
                        a_all[spot], b_own[m], (((1,), (1,)), ((), ())), preferred_element_type=jnp.float32)
                    k_ref[pl.ds(base, own), m * own_b : (m + 1) * own_b] = jnp.exp2(
                        logits * exponent).astype(jnp.bfloat16)
            if fused:
                row_part(0, base, own)

        def items():
            return [
                (b_ref, lambda row: b_all.at[1, row]),
                (down_ref.at[0:cut], lambda row: d_pair.at[row, 0:cut]),
                (down_ref.at[cut:cols], lambda row: d_pair.at[row, cut:cols]),
            ]

        hops, turns, cores = [], {}, {}

        def to_partner():
            for n, (src, dst) in enumerate(items()):
                hops.append(remote(src, dst(me_row), hs.at[n], hr.at[n], "col", partner))

        def core_sends(n, j, row):
            ref = items()[n][1](row)
            for i in range(1, row_inner):
                cores[n, j, i] = remote(ref, ref, ks.at[n, j, i], kr.at[n, j, i], "row",
                                        ro * row_inner + lax.rem(ri + i, row_inner))

        def relay(n):
            hops[n].wait_recv()
            ref = items()[n][1](me_row)
            for j in range(1, row_outer):
                turns[n, j] = remote(ref, ref, ys.at[n, j], yr.at[n, j], "row",
                                     lax.rem(ro + j, row_outer) * row_inner + ri)
            core_sends(n, 0, me_row)

        def spread(n):
            for j in range(1, row_outer):
                turns[n, j].wait_recv()
                core_sends(n, j, lax.rem(ro + row_outer - j, row_outer) * row_inner + ri)

        pass_on(1)
        keep_a.wait()
        keep_b.wait()
        for copy in gather_b:
            copy.wait_recv()
        for m in range(n_row):
            pltpu.make_async_copy(b_own.at[m], b_all.at[0, m], local.at[2 + m]).start()
        build(me_col)
        for i in range(1, inner):
            across[0, i].wait_recv()
            build(source(0, i))
        for j in range(2, outer):
            pass_on(j)
            if j == outer - 1:
                to_partner()
            build(source(j - 1, 0))
        build(source(outer - 1, 0))
        for j in range(1, outer):
            for i in range(1, inner):
                across[j, i].wait_recv()
                build(source(j, i))
        side = mo // (outer // 2)
        half_a = pltpu.make_async_copy(
            a_all.at[pl.ds(side * (n_col // 2), n_col // 2)], a_out, local.at[2 + n_row])
        half_a.start()

        def swap(step, send, recv, ssem, rsem, axis, me, n):
            copies = [
                remote(send.at[step], recv.at[step, j], ssem.at[step, j], rsem.at[step, j], axis, lax.rem(me + j, n))
                for j in range(1, n)
            ]
            total = send[step]
            for j, copy in enumerate(copies):
                copy.wait()
                total = total + recv[step, j + 1]
            return 1.0 / total

        for step in range(ITERS):
            if step or not fused:
                @pl.loop(0, rows // block)
                def _(i):
                    row_part(step, pl.multiple_of(i * block, block), block)
            scale = swap(step, r_send, r_recv, rs, rr, "col", me_col, n_col)
            if step == 0:
                relay(0)
            if step == 1:
                relay(1)
                spread(0)
            if step == 2:
                spread(1)
                relay(2)
            rv[...] = halves_of(scale)
            if step == ITERS - 1:
                r_ref[...] = scale
            c_send[step] = jnp.zeros((1, cols), jnp.float32)

            @pl.loop(0, rows // block)
            def _(i):
                base = pl.multiple_of(i * block, block)
                part = jnp.dot(
                    rv[:, pl.ds(base, block)], k_ref[pl.ds(base, block), :], preferred_element_type=jnp.float32)
                c_send[step] += part[0:1] + part[1:2]

            scale = swap(step, c_send, c_recv, cs, cr, "row", me_row, n_row)
            if step < ITERS - 1:
                cv[...] = halves_of(scale)
        spread(2)
        pair[0] = scale
        pair_c = remote(pair.at[0], pair.at[1], hs.at[3], hr.at[3], "col", partner)
        pair_c.wait()
        c_ref[...] = pair[...]
        for copy in along + list(across.values()) + gather_b + hops + list(turns.values()):
            copy.wait_send()
        for copy in cores.values():
            copy.wait()
        half_a.wait()
        for m in range(n_row):
            pltpu.make_async_copy(b_own.at[m], b_all.at[0, m], local.at[2 + m]).wait()

    dma = pltpu.SemaphoreType.DMA
    vmem, hbm = pl.BlockSpec(memory_space=pltpu.VMEM), pl.BlockSpec(memory_space=pl.ANY)
    return pl.pallas_call(
        body,
        in_specs=[vmem, vmem, hbm],
        out_specs=[vmem, vmem, hbm, hbm, hbm],
        out_shape=[
            jax.ShapeDtypeStruct((1, rows), jnp.float32),
            jax.ShapeDtypeStruct((2, 1, cols), jnp.float32),
            jax.ShapeDtypeStruct((n_col // 2, own, depth), jnp.bfloat16),
            jax.ShapeDtypeStruct((2, n_row, own_b, depth), jnp.bfloat16),
            jax.ShapeDtypeStruct((n_row, cols, width), jnp.bfloat16),
        ],
        scratch_shapes=[
            pltpu.VMEM((rows, cols), jnp.bfloat16),
            pltpu.VMEM((n_col, own, depth), jnp.bfloat16),
            pltpu.VMEM((n_row, own_b, depth), jnp.bfloat16),
            pltpu.VMEM((16, rows), jnp.bfloat16),
            pltpu.VMEM((16, cols), jnp.bfloat16),
            pltpu.VMEM((ITERS, 1, rows), jnp.float32),
            pltpu.VMEM((ITERS, 1, cols), jnp.float32),
            pltpu.VMEM((ITERS, n_col, 1, rows), jnp.float32),
            pltpu.VMEM((ITERS, n_row, 1, cols), jnp.float32),
            pltpu.VMEM((2, 1, cols), jnp.float32),
            dma((ITERS, n_col)), dma((ITERS, n_col)), dma((ITERS, n_row)), dma((ITERS, n_row)),
            dma((n_row,)), dma((n_row,)), dma((outer,)), dma((outer,)),
            dma((outer, inner)), dma((outer, inner)),
            dma((4,)), dma((4,)), dma((3, row_outer)), dma((3, row_outer)),
            dma((3, row_outer, row_inner)), dma((3, row_outer, row_inner)), dma((3 + n_row,)),
        ],
        compiler_params=pltpu.CompilerParams(
            collective_id=1, has_side_effects=True, vmem_limit_bytes=67043328),
        cost_estimate=pl.CostEstimate(
            flops=2 * rows * cols * depth * 3, bytes_accessed=2 * (rows + cols) * depth, transcendentals=rows * cols),
        name="sinkhorn",
    )(mine_a, mine_b, down_b)


def join(scores_a, b_all, row_scale, col_scale, down_own, down_pair, down_a, n_col, exponent):
    half, depth = scores_a.shape
    rows = 2 * half
    cols = b_all.shape[1]
    quarters, _, width = down_own.shape
    window = quarters * width
    outer, inner = grid_of(n_col)
    near = outer // 2
    group = near * inner
    own = rows // n_col
    subs = 2
    piece = own // subs
    steps = group * subs
    sent = steps - subs
    chunk = lane_chunk(cols, 512)
    pieces = cols // chunk

    def body(a_hbm, b_hbm, r_ref, c_ref, own_hbm, pair_hbm, down_ref, out_ref, a_ref, b_ref, d_ref, total, plan,
             out_buf, in_buf, local, ssem, rsem):
        me = lax.axis_index("col")
        mo, mi = me // inner, lax.rem(me, inner)
        side, near_o = mo // near, lax.rem(mo, near)

        def place(j):
            oo = lax.rem(near_o + j // inner, near)
            ii = lax.rem(mi + lax.rem(j, inner), inner)
            return (side * near + oo) * inner + ii

        barrier = pltpu.get_barrier_semaphore()
        for j in range(1, group):
            pl.semaphore_signal(barrier, 1, device_id={"col": place(j)}, device_id_type=MESH)
        loads = [
            pltpu.make_async_copy(a_hbm, a_ref, local.at[0]),
            pltpu.make_async_copy(b_hbm, b_ref, local.at[1]),
            pltpu.make_async_copy(own_hbm, d_ref.at[0], local.at[2]),
            pltpu.make_async_copy(pair_hbm, d_ref.at[1], local.at[3]),
        ]
        for load in loads:
            load.start()
        for load in loads:
            load.wait()
        pl.semaphore_wait(barrier, group - 1)

        def copy_of(t, target):
            return pltpu.make_async_remote_copy(
                out_buf.at[t], in_buf.at[t], ssem.at[t], rsem.at[t],
                device_id={"col": target}, device_id_type=MESH)

        @pl.loop(0, steps)
        def _(t):
            j = (group - 1) - t // subs
            target = place(j)
            first = pl.multiple_of((target - side * group) * own + lax.rem(t, subs) * piece, math.gcd(piece, 128))
            total[...] = jnp.zeros_like(total)
            for s in range(2):
                @pl.loop(0, pieces)
                def _(k):
                    base = pl.multiple_of(k * chunk, chunk)
                    logits = lax.dot_general(
                        a_ref[pl.ds(first, piece), :], b_ref[s, pl.ds(base, chunk), :], (((1,), (1,)), ((), ())),
                        preferred_element_type=jnp.float32)
                    plan[...] = (jnp.exp2(logits * exponent) * c_ref[s, :, pl.ds(base, chunk)]).astype(jnp.bfloat16)
                    for q in range(quarters):
                        total[:, q * width : (q + 1) * width] += jnp.dot(
                            plan[...], d_ref[s, q, pl.ds(base, chunk), :], preferred_element_type=jnp.float32)
            spot = pl.multiple_of(target * own + lax.rem(t, subs) * piece, math.gcd(piece, 8))
            out_buf[t] = (total[...] * r_ref[pl.ds(spot, piece), :]).astype(jnp.bfloat16)

            @pl.when(t < sent)
            def _():
                copy_of(t, target).start()

        @pl.loop(0, subs)
        def _(u):
            summed = out_buf[sent + u].astype(jnp.float32)
            for g in range(group - 1):
                copy_of(g * subs + u, place(1)).wait_recv()
                summed = summed + in_buf[g * subs + u].astype(jnp.float32)
            spot = pl.ds(pl.multiple_of(u * piece, math.gcd(piece, 16)), piece)
            out_ref[spot, :] = ((down_ref[spot, :].astype(jnp.float32) + summed) * 0.5).astype(jnp.bfloat16)

        @pl.loop(0, sent)
        def _(t):
            copy_of(t, place((group - 1) - t // subs)).wait_send()

    dma = pltpu.SemaphoreType.DMA
    vmem, hbm = pl.BlockSpec(memory_space=pltpu.VMEM), pl.BlockSpec(memory_space=pl.ANY)
    return pl.pallas_call(
        body,
        in_specs=[hbm, hbm, vmem, vmem, hbm, hbm, vmem],
        out_specs=vmem,
        out_shape=jax.ShapeDtypeStruct((own, window), jnp.bfloat16),
        scratch_shapes=[
            pltpu.VMEM((half, depth), jnp.bfloat16),
            pltpu.VMEM((2, cols, depth), jnp.bfloat16),
            pltpu.VMEM((2, quarters, cols, width), jnp.bfloat16),
            pltpu.VMEM((piece, window), jnp.float32),
            pltpu.VMEM((piece, chunk), jnp.bfloat16),
            pltpu.VMEM((steps, piece, window), jnp.bfloat16),
            pltpu.VMEM((sent, piece, window), jnp.bfloat16),
            dma((4,)), dma((steps,)), dma((steps,)),
        ],
        compiler_params=pltpu.CompilerParams(
            collective_id=2, has_side_effects=True, vmem_limit_bytes=67043328),
        cost_estimate=pl.CostEstimate(
            flops=2 * rows * cols * (window + depth), bytes_accessed=8 * cols * window, transcendentals=rows * cols),
        name="join",
    )(scores_a, b_all, row_scale, col_scale, down_own, down_pair, down_a)


def reduced(gate_pre, up_pre, axis, parts):
    tokens, width = gate_pre.shape
    own = width // parts
    both = jnp.stack((gate_pre.astype(jnp.bfloat16), up_pre.astype(jnp.bfloat16)))
    both = both.reshape(2, tokens, parts, own).transpose(2, 0, 1, 3)
    return lax.psum_scatter(both, axis, scatter_dimension=0, tiled=False)


def scores_of(summed):
    summed = summed.astype(jnp.float32)
    return standardize(summed[0], summed[1]).T


def solution(mesh):
    n_row, n_col = mesh.shape["row"], mesh.shape["col"]

    def per_device(calib, gate_a, up_a, gate_b, up_b, down_a, down_b):
        width_a = gate_a.shape[0]
        width_b = gate_b.shape[0]
        inputs_a = lax.dynamic_slice_in_dim(calib, lax.axis_index("col") * width_a, width_a, 1)
        inputs_b = lax.dynamic_slice_in_dim(calib, lax.axis_index("row") * width_b, width_b, 1)
        gate_pre_a = jnp.dot(inputs_a, gate_a, preferred_element_type=jnp.float32)
        up_pre_a = jnp.dot(inputs_a, up_a, preferred_element_type=jnp.float32)
        gate_pre_b = jnp.dot(inputs_b, gate_b, preferred_element_type=jnp.float32)
        up_pre_b = jnp.dot(inputs_b, up_b, preferred_element_type=jnp.float32)
        mine_b = scores_of(reduced(gate_pre_b, up_pre_b, "row", n_row))
        mine_a = scores_of(reduced(gate_pre_a, up_pre_a, "col", n_col))
        down_own = lax.all_gather(down_b, "row")
        exponent = math.log2(math.e) / (calib.shape[0] * softness)
        row_scale, col_scale, a_half, b_all, down_pair = sinkhorn(mine_a, mine_b, down_b, n_row, n_col, exponent)
        depth = calib.shape[0]
        return join(
            a_half.reshape(-1, depth), b_all.reshape(2, -1, depth), row_scale.reshape(-1, 1), col_scale,
            down_own, down_pair, down_a, n_col, exponent)

    placed = (
        P(),
        P("col", "row"),
        P("col", "row"),
        P("row", "col"),
        P("row", "col"),
        P(("row", "col"), None),
        P("col", "row"),
    )
    return jax.shard_map(
        per_device, mesh=mesh, in_specs=placed, out_specs=P(("row", "col"), None), check_vma=False
    )
```
